32 devices in a mesh: dp: 8 (over z, y), cent: 4 (over x, core).
Axes of the slice: x: 2, y: 2, z: 4, core: 2. Of those that a mesh axis runs over, the one named last changes fastest.
Arguments:
- stream: bfloat16 [16384, 768], P('dp'), may hold values from -6 to 6
- sample_index: int32 [8192], P('dp'), may hold values from 0 to 2047
- centroids: float32 [16384, 768], P(('cent', 'dp')), may hold values from -6 to 6
- first_moment: float32 [16384, 768], P(('cent', 'dp')), may hold values from -3 to 3
- second_moment: float32 [16384, 768], P(('cent', 'dp')), may hold values from 0.01 to 1
Outputs:
- new_centroids: float32 [16384, 768], P(('cent', 'dp'))
- new_first: float32 [16384, 768], P(('cent', 'dp'))
- new_second: float32 [16384, 768], P(('cent', 'dp'))
The draws below stay inside these ranges and needn't reach their ends.
All inputs are finite; a program needn't handle non-finite values.
Results may differ from the reference program's by a relative error of at most 0.0003.
Values may be sent and summed in bfloat16 or wider, within the bound.
No kernel may reach another device: no remote copies, remote signals or barrier semaphores. Data moves between devices by JAX's collectives and lax.ppermute only.
A program may use at most 128 MiB of HBM per device.

```python
import math
import jax
import jax.numpy as jnp
from jax import lax

E = 768
KB = 16384
ND = 1024
ITERS = 3
ROWS = 8192
STREAM = 16384
N_DP = 8


def distant_rows(key):
    placed = jax.random.permutation(jax.random.fold_in(key, 11), KB)[:8].astype(jnp.int32)
    flips = jax.random.bernoulli(jax.random.fold_in(key, 12), 0.5, (8, E))
    signs = jnp.where(flips, 1.0, -1.0).astype(jnp.float32)
    levels = jnp.array([0.75, 1.0, 1.25, 1.5, 0.75, 1.0, 1.25, 1.5], jnp.float32) * jnp.sqrt(768.0 / E)
    return (placed, levels[:, None] * signs)


def draw_stream(key, part):
    drawn_values = jnp.clip(jax.random.normal(jax.random.fold_in(key, 1), (STREAM, E), jnp.float32), -6.0, 6.0)
    return drawn_values.astype(jnp.bfloat16)


def draw_centroids(key, part):
    drawn_values = jnp.clip(0.1 * jax.random.normal(jax.random.fold_in(key, 2), (KB, E), jnp.float32), -0.6, 0.6)
    placed, distant = distant_rows(key)
    drawn_values = drawn_values.at[placed].set(distant)
    return drawn_values


def touch_ends(drawn, stream_key, low, largest):
    longest = drawn.shape.index(max(drawn.shape))
    spots = []
    for shift in (0, 1):
        where = [jax.random.randint(jax.random.fold_in(stream_key, axis), (), 0, length) for axis, length in enumerate(drawn.shape)]
        where[longest] = (where[longest] + shift) % drawn.shape[longest]
        spots.append(tuple(where))
    return drawn.at[spots[0]].set(low).at[spots[1]].set(largest)


def steps_of(own_key, shape, split, low, top_value):
    def one(dim, shards_of):
        heights = jax.random.uniform(jax.random.fold_in(jax.random.fold_in(own_key, 6), dim), (shards_of,), jnp.float32, low / len(split), top_value / len(split))
        return jnp.repeat(jnp.exp(heights), shape[dim] // shards_of).reshape((-1,) + (1,) * (len(shape) - dim - 1))

    level = one(*split[0])
    for cut in split[1:]:
        level = level * one(*cut)
    return level


def noise(own_key, dims, scale, limit, pieces=(), kind=jnp.bfloat16):
    values = scale * jax.random.normal(own_key, dims, jnp.float32)
    if pieces:
        values = values * steps_of(own_key, dims, pieces, -0.22, 0.18)
    return jnp.clip(values, -limit, limit).astype(kind)


def setup_inputs(seed: int = 0) -> dict:
    streams_of = jax.random.split(jax.random.key(seed), 6)
    stream = draw_stream(jax.random.fold_in(streams_of[5], 71), 0)
    sample_index = touch_ends(jax.random.randint(streams_of[1], (ROWS,), 0, 2 * ND), jax.random.fold_in(streams_of[1], 1), 0, (2 * ND) - 1).astype(jnp.int32)
    centroids = draw_centroids(jax.random.fold_in(streams_of[5], 71), 0)
    first_moment = noise(streams_of[3], (KB, E), 0.5, 3.0, ((0, 32),), jnp.float32)
    second_moment = jnp.clip(jnp.exp(math.log(1.0) - 4.6051702 * jax.random.uniform(streams_of[4], (KB, E), jnp.float32) ** steps_of(streams_of[4], (KB, E), ((0, 32),), -0.2, 0.2)), 0.01, 1.0)
    return {"stream": stream, "sample_index": sample_index, "centroids": centroids, "first_moment": first_moment, "second_moment": second_moment}


temper = 2.0
beta_one = 0.9
beta_two = 0.99
step_rate = 0.05
epsilon = 1e-08

def logits_of(row_block, rounded, squares):
    product = jnp.dot(row_block, rounded.T, preferred_element_type=jnp.float32)
    return (2.0 * product - squares[None, :]) / temper

def row_potential(logits, column_pot):
    shifted = logits + column_pot[None, :]
    highest = lax.optimization_barrier(jnp.max(shifted, axis=1))
    return -(highest + jnp.log(lax.optimization_barrier(jnp.sum(jnp.exp(shifted - highest[:, None]), axis=1))))

def reference(stream, sample_index, centroids, first_moment, second_moment):
    row_ids = jnp.arange(ROWS, dtype=jnp.int32)
    global_rows = (row_ids // ND * (2 * ND) + sample_index).astype(jnp.int32)
    embedded = stream[global_rows].reshape(N_DP, ND, E)
    rounded = centroids.astype(jnp.bfloat16)
    squares = lax.optimization_barrier(jnp.sum(rounded.astype(jnp.float32) ** 2, axis=1))
    balance = math.log(ROWS / KB)

    def column_pass(column_pot):

        def visit(running, row_block):
            logits = logits_of(row_block, rounded, squares)
            row_pot = row_potential(logits, column_pot)
            shifted = logits + row_pot[:, None]
            highest = lax.optimization_barrier(jnp.max(shifted, axis=0))
            summed = lax.optimization_barrier(jnp.sum(jnp.exp(shifted - highest[None, :]), axis=0))
            merged_peak = jnp.maximum(running[0], highest)
            merged_total = running[1] * jnp.exp(running[0] - merged_peak) + summed * jnp.exp(highest - merged_peak)
            return ((merged_peak, merged_total), None)
        initial = (jnp.full((KB,), -1e+30, jnp.float32), jnp.zeros((KB,), jnp.float32))
        (highest, summed), _ = lax.scan(visit, initial, embedded)
        return balance - (highest + jnp.log(summed))
    column_pot = jnp.zeros((KB,), jnp.float32)
    for sweep_index in range(ITERS):
        column_pot = column_pass(column_pot)

    def gather_stats(running, row_block):
        logits = logits_of(row_block, rounded, squares)
        row_pot = row_potential(logits, column_pot)
        transport = jnp.exp(logits + row_pot[:, None] + column_pot[None, :]).astype(jnp.bfloat16)
        weighted = running[0] + jnp.dot(transport.T, row_block, preferred_element_type=jnp.float32)
        weight_mass = running[1] + lax.optimization_barrier(jnp.sum(transport.astype(jnp.float32), axis=0))
        return ((weighted, weight_mass), None)
    initial = (jnp.zeros((KB, E), jnp.float32), jnp.zeros((KB,), jnp.float32))
    (weighted, weight_mass), _ = lax.scan(gather_stats, initial, embedded)
    gradient = (weight_mass[:, None] * centroids - weighted) * (KB / ROWS)
    new_first = beta_one * first_moment + (1.0 - beta_one) * gradient
    new_second = beta_two * second_moment + (1.0 - beta_two) * gradient * gradient
    new_centroids = centroids - step_rate * new_first / (jnp.sqrt(new_second) + epsilon)
    return (new_centroids, new_first, new_second)
```

```python
import functools
import math

import jax
import jax.numpy as jnp
from jax import lax
from jax.experimental import pallas as pl
from jax.experimental.pallas import tpu as pltpu
from jax.sharding import PartitionSpec as P

ITERS = 3

temper = 2.0
beta_one = 0.9
beta_two = 0.99
step_rate = 0.05
epsilon = 1e-08

LOG2E = math.log2(math.e)
MIB = 1 << 20


def scores_kernel(own_rows, where_ref, *refs):
    if own_rows:
        rows_ref, c_ref, sq_ref, emb_out, logit_out, lse_out = refs
        emb_out[...] = rows_ref[...]
    else:
        a0, x0, a1, x1, c_ref, sq_ref, _, _, _, emb_out, logit_out, lse_out = refs
        a, p = a0.shape[0], x0.shape[0]
        half = a + p
        x, c = where_ref[1], where_ref[2]
        for core, near, far in ((c, a0, x0), (1 - c, a1, x1)):
            base = core * half
            emb_out[pl.ds(pl.multiple_of(base + x * p, 16), a), :] = near[...]
            emb_out[pl.ds(pl.multiple_of(base + (1 - x) * a, 16), p), :] = far[...]
    n = emb_out.shape[0]
    tile = 256
    cents = c_ref[...]
    sq = sq_ref[...]
    for t in range(n // tile):
        rows = emb_out[t * tile : (t + 1) * tile, :]
        product = lax.dot_general(cents, rows, (((1,), (1,)), ((), ())), preferred_element_type=jnp.float32)
        logits = (product - sq) * LOG2E
        logit_out[:, t * tile : (t + 1) * tile] = logits
        highest = jnp.max(logits, axis=0, keepdims=True)
        summed = jnp.sum(jnp.exp2(logits - highest), axis=0, keepdims=True)
        lse_out[:, t * tile : (t + 1) * tile] = highest + jnp.log2(summed)


def scores(pieces, where, cents, sq, total, held=()):
    cols, width = cents.shape
    own_rows = len(pieces) == 1
    n = pieces[0].shape[0] if own_rows else 2 * (pieces[0].shape[0] + pieces[1].shape[0])
    full = lambda shape: pl.BlockSpec(shape, lambda i, w: (0, 0))
    anywhere = pl.BlockSpec(memory_space=pl.ANY)
    np_ = len(pieces)
    return pl.pallas_call(
        functools.partial(scores_kernel, own_rows),
        grid_spec=pltpu.PrefetchScalarGridSpec(
            num_scalar_prefetch=1,
            grid=(1,),
            in_specs=[full(q.shape) for q in pieces] + [full(cents.shape), full(sq.shape)] + [anywhere] * len(held),
            out_specs=[
                pl.BlockSpec((n, width), lambda i, w: (w[0], 0)),
                pl.BlockSpec((cols, n), lambda i, w: (0, w[0])),
                pl.BlockSpec((1, n), lambda i, w: (0, w[0])),
            ],
        ),
        out_shape=[
            jax.ShapeDtypeStruct((total, width), jnp.bfloat16),
            jax.ShapeDtypeStruct((cols, total), jnp.float32),
            jax.ShapeDtypeStruct((1, total), jnp.float32),
        ],
        input_output_aliases={np_ + 3 + i: i for i in range(len(held))},
        compiler_params=pltpu.CompilerParams(vmem_limit_bytes=24 * MIB),
        cost_estimate=pl.CostEstimate(
            flops=2 * cols * n * width, bytes_accessed=4 * cols * n + 4 * n * width + 2 * cols * width, transcendentals=cols * n
        ),
        name="scores",
    )(where, *pieces, cents, sq, *held)


def balance_kernel(first, share, logit_ref, u_ref, v_ref, v_out, r_out, p_ref, r_acc):
    step = pl.program_id(0)
    cols, total = logit_ref.shape
    lanes = 512
    groups = cols // 8

    @pl.when(step == 0)
    def _():
        r_acc[...] = jnp.zeros_like(r_acc)

    if first:
        top = jnp.full((cols, 128), -jnp.inf, jnp.float32)

        def peak(t, top):
            for k in range(lanes // 128):
                at = pl.ds(pl.multiple_of(t * lanes + k * 128, 128), 128)
                top = jnp.maximum(top, logit_ref[:, at] + u_ref[:, at])
            return top

        top = lax.fori_loop(0, total // lanes, peak, top)
        shift = -jnp.max(top, axis=1, keepdims=True)
    else:
        shift = v_ref[...]
    wide = jnp.broadcast_to(shift, (cols, 128))

    def weigh(t, acc):
        for k in range(lanes // 128):
            at = pl.ds(pl.multiple_of(t * lanes + k * 128, 128), 128)
            value = jnp.exp2(logit_ref[:, at] + (u_ref[:, at] + wide))
            p_ref[:, at] = value
            acc = acc + value
        return acc

    acc = lax.fori_loop(0, total // lanes, weigh, jnp.zeros((cols, 128), jnp.float32))
    summed = jnp.sum(acc, axis=1, keepdims=True)
    v_out[...] = shift + (share - jnp.log2(summed))
    factor = jnp.broadcast_to(2.0**share / summed, (cols, 128))

    def fold(t, carry):
        for k in range(lanes // 128):
            at = pl.ds(pl.multiple_of(t * lanes + k * 128, 128), 128)
            scaled = p_ref[:, at] * factor
            part = scaled[0:8]
            for g in range(1, groups):
                part = part + scaled[g * 8 : g * 8 + 8]
            r_acc[:, at] = r_acc[:, at] + part
        return carry

    lax.fori_loop(0, total // lanes, fold, 0)

    @pl.when(step == pl.num_programs(0) - 1)
    def _():
        r_out[...] = jnp.sum(r_acc[...], axis=0, keepdims=True)


def balance(first, share, logits, u, v):
    cols, total = logits.shape
    block = 64
    return pl.pallas_call(
        functools.partial(balance_kernel, first, share),
        grid=(cols // block,),
        in_specs=[
            pl.BlockSpec((block, total), lambda i: (i, 0)),
            pl.BlockSpec((1, total), lambda i: (0, 0)),
            pl.BlockSpec((block, 1), lambda i: (i, 0)),
        ],
        out_specs=[pl.BlockSpec((block, 1), lambda i: (i, 0)), pl.BlockSpec((1, total), lambda i: (0, 0))],
        out_shape=[jax.ShapeDtypeStruct((cols, 1), jnp.float32), jax.ShapeDtypeStruct((1, total), jnp.float32)],
        scratch_shapes=[pltpu.VMEM((block, total), jnp.float32), pltpu.VMEM((8, total), jnp.float32)],
        compiler_params=pltpu.CompilerParams(vmem_limit_bytes=24 * MIB),
        cost_estimate=pl.CostEstimate(flops=6 * cols * total, bytes_accessed=4 * cols * total, transcendentals=cols * total),
        name="balance",
    )(logits, u, v)


def update_kernel(gain, logit_ref, emb_ref, u_ref, v_ref, c_ref, m_ref, s_ref, c_out, m_out, s_out, acc, mass):
    step = pl.program_id(0)

    @pl.when(step == 0)
    def _():
        acc[...] = jnp.zeros_like(acc)
        mass[...] = jnp.zeros_like(mass)

    transport = jnp.exp2(logit_ref[...] + u_ref[...] + v_ref[...]).astype(jnp.bfloat16)
    acc[...] += jnp.dot(transport, emb_ref[...], preferred_element_type=jnp.float32)
    mass[...] += jnp.sum(transport.astype(jnp.float32), axis=1, keepdims=True)

    @pl.when(step == pl.num_programs(0) - 1)
    def _():
        cents = c_ref[...]
        gradient = (mass[...] * cents - acc[...]) * gain
        new_first = beta_one * m_ref[...] + (1.0 - beta_one) * gradient
        new_second = beta_two * s_ref[...] + (1.0 - beta_two) * gradient * gradient
        m_out[...] = new_first
        s_out[...] = new_second
        c_out[...] = cents - step_rate * new_first / (jnp.sqrt(new_second) + epsilon)


def update(gain, logits, emb, u, v, centroids, first_moment, second_moment):
    cols, total = logits.shape
    width = emb.shape[1]
    block = 512
    whole = pl.BlockSpec((cols, width), lambda i: (0, 0))
    out = jax.ShapeDtypeStruct((cols, width), jnp.float32)
    return pl.pallas_call(
        functools.partial(update_kernel, gain),
        grid=(total // block,),
        in_specs=[
            pl.BlockSpec((cols, block), lambda i: (0, i)),
            pl.BlockSpec((block, width), lambda i: (i, 0)),
            pl.BlockSpec((1, block), lambda i: (0, i)),
            pl.BlockSpec((cols, 1), lambda i: (0, 0)),
            whole,
            whole,
            whole,
        ],
        out_specs=[whole, whole, whole],
        out_shape=[out, out, out],
        scratch_shapes=[pltpu.VMEM((cols, width), jnp.float32), pltpu.VMEM((cols, 1), jnp.float32)],
        compiler_params=pltpu.CompilerParams(vmem_limit_bytes=40 * MIB),
        cost_estimate=pl.CostEstimate(
            flops=2 * cols * total * width, bytes_accessed=4 * cols * total + 2 * total * width + 24 * cols * width, transcendentals=cols * total
        ),
        name="update",
    )(logits, emb, u, v, centroids, first_moment, second_moment)


def over(axis, size, mask):
    return functools.partial(lax.ppermute, axis_name=axis, perm=[(i, i ^ mask) for i in range(size)])


def all_sum(value, dp, combine):
    value = combine([value, over("cent", 4, 1)(value)])
    plane = [value, over("cent", 4, 2)(value), over("dp", dp, 1)(value)]
    both = lax.ppermute(value, ("dp", "cent"), [(d * 4 + k, (d ^ 1) * 4 + (k ^ 2)) for d in range(dp) for k in range(4)])
    value = combine(plane + [both])
    line = [value] + [over("dp", dp, 2 * m)(value) for m in range(1, dp // 2)]
    return combine(line)


def add_up(parts):
    return functools.reduce(lambda a, b: a + b, parts)


def log_add_up(parts):
    top = functools.reduce(jnp.maximum, parts)
    return top + jnp.log2(add_up([jnp.exp2(q - top) for q in parts]))


def gathered(stream, sample_index, centroids, first_moment, second_moment):
    dp, cent = lax.axis_size("dp"), lax.axis_size("cent")
    local = sample_index.shape[0]
    width = stream.shape[1]
    cols = centroids.shape[0]
    total = local * dp
    band = cols * dp * cent
    half = local // 2
    p = (half * 11 // 32) // 16 * 16
    a = half - p
    d, k = lax.axis_index("dp"), lax.axis_index("cent")
    x, c = k // 2, k % 2
    z, inner = d // 2, d % 2

    def take(index):
        return stream.at[index].get(mode="promise_in_bounds")

    mine = take(lax.dynamic_slice(sample_index, (c * half + x * p,), (a,)))
    line = dp // 2
    up = functools.partial(lax.ppermute, axis_name="dp", perm=[(i, i + 2) for i in range(dp - 2)])
    down = functools.partial(lax.ppermute, axis_name="dp", perm=[(i + 2, i) for i in range(dp - 2)])
    side, across, core = over("dp", dp, 1), over("cent", cent, 2), over("cent", cent, 1)

    def far_part(piece):
        return lax.dynamic_slice(piece, (x * (a - p), 0), (p, width))

    rounded = centroids.astype(jnp.bfloat16)
    sq = jnp.sum(rounded.astype(jnp.float32) ** 2, axis=1, keepdims=True) / temper

    y0 = side(mine)
    u1, d1 = up(mine), down(mine)
    own = take(sample_index)
    held = scores([own], jnp.stack([d, x, c]), rounded, sq, total)
    low = z < 2
    q1 = jnp.where(low, d1, u1)
    y1 = side(q1)
    u2, d2 = up(u1), down(d1)
    q2 = jnp.where(z == 0, d2, jnp.where(z == 1, u1, jnp.where(z == 2, d1, u2)))
    y2 = side(q2)
    u3, d3 = up(u2), down(d2)
    q3 = jnp.where(z == 0, d3, jnp.where(z == 1, d2, jnp.where(z == 2, u2, u3)))
    y3 = side(q3)
    from1 = jnp.where(low, z + 1, z - 1)
    from2 = jnp.where(z == 0, 2, jnp.where(z == 1, 0, jnp.where(z == 2, 3, 1)))
    from3 = jnp.where(low, 3, 0)
    order = [
        (y0, z, 1 - inner),
        (q1, from1, inner),
        (y1, from1, 1 - inner),
        (q2, from2, inner),
        (y2, from2, 1 - inner),
        (q3, from3, inner),
        (y3, from3, 1 - inner),
    ]
    for piece, sz, sy in order:
        far = across(far_part(piece))
        pieces = [piece, far, core(piece), core(far)]
        held = scores(pieces, jnp.stack([sz * 2 + sy, x, c]), rounded, sq, total, held)

    emb, logits, lse = held
    share = math.log2(total / band)
    u = -all_sum(lse.reshape(total), dp, log_add_up)
    v = jnp.zeros((cols, 1), jnp.float32)
    for sweep in range(ITERS):
        v, r = balance(sweep == 0, share, logits, u.reshape(1, total), v)
        u = u - jnp.log2(all_sum(r.reshape(total), dp, add_up))
    return tuple(update(band / total, logits, emb, u.reshape(1, total), v, centroids, first_moment, second_moment))


def scattered(stream, sample_index, centroids, first_moment, second_moment):
    embedded = stream[sample_index]
    total_rows = embedded.shape[0] * lax.axis_size("dp")
    band = centroids.shape[0] * lax.axis_size("dp") * lax.axis_size("cent")
    balance_of = math.log(total_rows / band)
    rounded = centroids.astype(jnp.bfloat16)
    shard_piece = lax.all_gather(rounded, "dp", axis=0, tiled=True)
    squares = jnp.sum(shard_piece.astype(jnp.float32) ** 2, axis=1)
    product = lax.dot_general(embedded, shard_piece, (((1,), (1,)), ((), ())), preferred_element_type=jnp.float32)
    logits = (2.0 * product - squares[None, :]) / temper

    def potential(shifted, axis, name):
        highest = jnp.max(shifted, axis=axis, keepdims=True)
        summed = jnp.sum(jnp.exp(shifted - highest), axis=axis, keepdims=True)
        overall = lax.pmax(highest, name)
        return -(overall + jnp.log(lax.psum(summed * jnp.exp(highest - overall), name)))

    column_pot = jnp.zeros((1, logits.shape[1]), jnp.float32)
    for _ in range(ITERS):
        row_pot = potential(logits + column_pot, 1, "cent")
        column_pot = balance_of + potential(logits + row_pot, 0, "dp")
    row_pot = potential(logits + column_pot, 1, "cent")
    transport = jnp.exp(logits + row_pot + column_pot).astype(jnp.bfloat16)
    weighted = lax.dot_general(transport, embedded, (((0,), (0,)), ((), ())), preferred_element_type=jnp.float32)
    weight_mass = jnp.sum(transport.astype(jnp.float32), axis=0)
    weighted = lax.psum_scatter(weighted, "dp", scatter_dimension=0, tiled=True)
    weight_mass = lax.psum_scatter(weight_mass, "dp", scatter_dimension=0, tiled=True)
    gradient = (weight_mass[:, None] * centroids - weighted) * (band / total_rows)
    new_first = beta_one * first_moment + (1.0 - beta_one) * gradient
    new_second = beta_two * second_moment + (1.0 - beta_two) * gradient * gradient
    new_centroids = centroids - step_rate * new_first / (jnp.sqrt(new_second) + epsilon)
    return (new_centroids, new_first, new_second)


def solution(mesh):
    small = mesh.shape["dp"] == 8 and mesh.shape["cent"] == 4
    return jax.shard_map(
        gathered if small else scattered,
        mesh=mesh,
        in_specs=(
            P("dp", None),
            P("dp"),
            P(("cent", "dp"), None),
            P(("cent", "dp"), None),
            P(("cent", "dp"), None),
        ),
        out_specs=(P(("cent", "dp"), None), P(("cent", "dp"), None), P(("cent", "dp"), None)),
        check_vma=False,
    )
```

```python
import functools
import math

import jax
import jax.numpy as jnp
from jax import lax
from jax.experimental import pallas as pl
from jax.experimental.pallas import tpu as pltpu
from jax.sharding import PartitionSpec as P

ITERS = 3

temper = 2.0
beta_one = 0.9
beta_two = 0.99
step_rate = 0.05
epsilon = 1e-08

LOG2E = math.log2(math.e)
MIB = 1 << 20


IN_VMEM = pl.BlockSpec(memory_space=pltpu.VMEM)
ANYWHERE = pl.BlockSpec(memory_space=pl.ANY)
LANES = 128


def in_vmem(value):
    return pltpu.with_memory_space_constraint(value, pltpu.VMEM)


def in_hbm(value):
    return pltpu.with_memory_space_constraint(value, pltpu.HBM)


def scores_kernel(segments, half, p, where_ref, *refs):
    count = 1 + max(segment[0] for segment in segments)
    pieces, (c_ref, sq_ref) = refs[:count], refs[count : count + 2]
    emb_out, logit_out, lse_out, rows_ref = refs[-4:]
    shard, tile = pl.program_id(0), pl.program_id(1)
    x, c = where_ref[2], where_ref[3]

    def place(number):
        for piece, start, rows, to, sibling, kind in segments:
            if to == number:
                if kind == "whole":
                    rows_ref[...] = pieces[piece][...]
                    continue
                core = 1 - c if sibling else c
                inside = {"near": x * p, "far": (1 - x) * p, "shared": 2 * p}[kind]
                at = pl.ds(pl.multiple_of(core * half + inside, 16), rows)
                rows_ref[at, :] = pieces[piece][start : start + rows, :]

    for number in range(1 + max(segment[3] for segment in segments)):
        pl.when(jnp.logical_and(tile == 0, shard == number))(functools.partial(place, number))
    n = emb_out.shape[0]
    rows = rows_ref[pl.ds(pl.multiple_of(tile * n, n), n), :]
    emb_out[...] = rows
    product = lax.dot_general(c_ref[...], rows, (((1,), (1,)), ((), ())), preferred_element_type=jnp.float32)
    logits = (product - sq_ref[...]) * LOG2E
    logit_out[...] = logits
    highest = jnp.max(logits, axis=0, keepdims=True)
    summed = jnp.sum(jnp.exp2(logits - highest), axis=0, keepdims=True)
    lse_out[...] = highest + jnp.log2(summed)


def scores(pieces, segments, where, half, p, cents, sq, total, held=()):
    cols, width = cents.shape
    shards = 1 + max(segment[3] for segment in segments)
    n = min(256, half)
    tiles = 2 * half // n
    full = lambda shape: pl.BlockSpec(shape, lambda s, t, w: (0, 0))
    first = len(pieces) + 3
    return pl.pallas_call(
        functools.partial(scores_kernel, segments, half, p),
        grid_spec=pltpu.PrefetchScalarGridSpec(
            num_scalar_prefetch=1,
            grid=(shards, tiles),
            in_specs=[full(q.shape) for q in pieces] + [full(cents.shape), full(sq.shape)] + [ANYWHERE] * len(held),
            out_specs=[
                pl.BlockSpec((n, width), lambda s, t, w: (w[s] * tiles + t, 0)),
                pl.BlockSpec((cols, n), lambda s, t, w: (0, w[s] * tiles + t)),
                pl.BlockSpec((1, n), lambda s, t, w: (0, w[s] * tiles + t)),
            ],
            scratch_shapes=[pltpu.VMEM((2 * half, width), jnp.bfloat16)],
        ),
        out_shape=[
            pltpu.HBM((total, width), jnp.bfloat16),
            pltpu.HBM((cols, total), jnp.float32),
            pltpu.HBM((1, total), jnp.float32),
        ],
        input_output_aliases={first + i: i for i in range(len(held))},
        compiler_params=pltpu.CompilerParams(vmem_limit_bytes=24 * MIB),
        cost_estimate=pl.CostEstimate(
            flops=4 * cols * shards * half * width,
            bytes_accessed=8 * (cols + width) * shards * half,
            transcendentals=2 * cols * shards * half,
        ),
        name="scores",
    )(where, *pieces, cents, sq, *map(in_hbm, held))


def balance_kernel(first, keep, share, logit_ref, u_ref, v_ref, v_out, r_out, *refs):
    kept = refs[0]
    p_ref, r_acc = refs[-2:] if not first else refs[-3:-1]
    cols, total = logit_ref.shape
    block = p_ref.shape[0]
    tiles = total // LANES
    r_acc[...] = jnp.zeros_like(r_acc)

    def lanes(t):
        return pl.ds(pl.multiple_of(t * LANES, LANES), LANES)

    def brought(b):
        rows = pl.ds(pl.multiple_of(b * block, block), block)
        return pltpu.make_async_copy(logit_ref.at[rows, :], kept.at[rows, :], refs[-1].at[b])

    if first:
        for b in range(cols // block):
            brought(b).start()
        logit_ref_now = kept
    else:
        logit_ref_now = logit_ref

    def part(b, carry):
        rows = pl.ds(pl.multiple_of(b * block, block), block)
        if first:
            brought(b).wait()

            def peak(t, top):
                return jnp.maximum(top, logit_ref_now[rows, lanes(t)] + u_ref[:, lanes(t)])

            top = lax.fori_loop(0, tiles, peak, jnp.full((block, LANES), -jnp.inf, jnp.float32), unroll=8)
            shift = -jnp.max(top, axis=1, keepdims=True)
        else:
            shift = v_ref[rows, :]
        wide = jnp.broadcast_to(shift, (block, LANES))

        def weigh(t, acc):
            value = jnp.exp2((logit_ref_now[rows, lanes(t)] + u_ref[:, lanes(t)]) + wide)
            p_ref[:, lanes(t)] = value
            return acc + value

        acc = lax.fori_loop(0, tiles, weigh, jnp.zeros((block, LANES), jnp.float32), unroll=8)
        summed = jnp.sum(acc, axis=1, keepdims=True)
        v_out[rows, :] = shift + (share - jnp.log2(summed))
        factor = jnp.broadcast_to(2.0**share / summed, (block, LANES))

        def fold(t, carry):
            scaled = p_ref[:, lanes(t)] * factor
            if keep:
                kept[rows, lanes(t)] = scaled
            parts = [scaled[g : g + 8] for g in range(0, block, 8)] + [r_acc[:, lanes(t)]]
            while len(parts) > 1:
                parts = [i + j for i, j in zip(parts[::2], parts[1::2])] + parts[len(parts) // 2 * 2 :]
            r_acc[:, lanes(t)] = parts[0]
            return carry

        lax.fori_loop(0, tiles, fold, 0, unroll=8)
        return carry

    lax.fori_loop(0, cols // block, part, 0)
    r_out[...] = jnp.sum(r_acc[...], axis=0, keepdims=True)


def balance(first, keep, share, logits, u, v):
    cols, total = logits.shape
    block = min(64 if first else 128, cols)
    held = first or keep
    scratch = [pltpu.VMEM((block, total), jnp.float32), pltpu.VMEM((8, total), jnp.float32)]
    return pl.pallas_call(
        functools.partial(balance_kernel, first, keep, share),
        in_specs=[ANYWHERE if first else IN_VMEM] + [IN_VMEM] * 2,
        out_specs=[IN_VMEM] * (3 if held else 2),
        out_shape=[jax.ShapeDtypeStruct((cols, 1), jnp.float32), jax.ShapeDtypeStruct((1, total), jnp.float32)]
        + ([pltpu.VMEM((cols, total), jnp.float32)] if held else []),
        scratch_shapes=scratch + ([pltpu.SemaphoreType.DMA((cols // block,))] if first else []),
        input_output_aliases={} if first or not keep else {0: 2},
        compiler_params=pltpu.CompilerParams(vmem_limit_bytes=40 * MIB),
        cost_estimate=pl.CostEstimate(flops=6 * cols * total, bytes_accessed=4 * total, transcendentals=cols * total),
        name="balance",
    )(in_hbm(logits) if first else in_vmem(logits), u, v)


def update_kernel(gain, t_ref, emb_hbm, a_ref, c_hbm, m_hbm, s_hbm, c_out, m_out, s_out, acc, mass, slots, emb_ref, c_ref, m_ref, s_ref, sems):
    cols, total = t_ref.shape
    block = slots.shape[2]
    steps = total // block

    def brought(step):
        rows = pl.ds(pl.multiple_of(step * block, block), block)
        return pltpu.make_async_copy(emb_hbm.at[rows, :], emb_ref.at[rows, :], sems.at[step])

    for step in range(steps):
        brought(step).start()
    moments = [
        pltpu.make_async_copy(source, target, sems.at[steps + i])
        for i, (source, target) in enumerate(((c_hbm, c_ref), (m_hbm, m_ref), (s_hbm, s_ref)))
    ]
    for moment in moments:
        moment.start()

    def weigh(step, slot):
        for g in range(0, cols, 64):
            total_of = mass[g : g + 64, :]
            for t in range(block // LANES):
                at = pl.ds(pl.multiple_of(step * block + t * LANES, LANES), LANES)
                value = (t_ref[g : g + 64, at] * a_ref[:, at]).astype(jnp.bfloat16)
                slots[slot, g : g + 64, t * LANES : (t + 1) * LANES] = value
                total_of = total_of + value.astype(jnp.float32)
            mass[g : g + 64, :] = total_of

    mass[...] = jnp.zeros_like(mass)
    acc[...] = jnp.zeros_like(acc)
    weigh(0, 0)

    def product(step):
        rows = pl.ds(pl.multiple_of(step * block, block), block)
        acc[...] += jnp.dot(slots[lax.rem(step, 2)], emb_ref[rows, :], preferred_element_type=jnp.float32)

    def both(step, carry):
        brought(step).wait()
        weigh(step + 1, lax.rem(step + 1, 2))
        product(step)
        return carry

    lax.fori_loop(0, steps - 1, both, 0)
    brought(steps - 1).wait()
    product(steps - 1)
    for moment in moments:
        moment.wait()
    cents = c_ref[...]
    gradient = (jnp.sum(mass[...], axis=1, keepdims=True) * cents - acc[...]) * gain
    new_first = beta_one * m_ref[...] + (1.0 - beta_one) * gradient
    new_second = beta_two * s_ref[...] + (1.0 - beta_two) * gradient * gradient
    m_out[...] = new_first
    s_out[...] = new_second
    c_out[...] = cents - step_rate * new_first / (jnp.sqrt(new_second) + epsilon)


def update(gain, transport, emb, scale, centroids, first_moment, second_moment):
    cols, total = transport.shape
    width = emb.shape[1]
    block = min(1024, total)
    out = jax.ShapeDtypeStruct((cols, width), jnp.float32)
    return pl.pallas_call(
        functools.partial(update_kernel, gain),
        in_specs=[IN_VMEM, ANYWHERE, IN_VMEM] + [ANYWHERE] * 3,
        out_specs=[IN_VMEM] * 3,
        out_shape=[out, out, out],
        scratch_shapes=[
            pltpu.VMEM((cols, width), jnp.float32),
            pltpu.VMEM((cols, LANES), jnp.float32),
            pltpu.VMEM((2, cols, block), jnp.bfloat16),
            pltpu.VMEM((total, width), jnp.bfloat16),
            *[pltpu.VMEM((cols, width), jnp.float32)] * 3,
            pltpu.SemaphoreType.DMA((total // block + 3,)),
        ],
        compiler_params=pltpu.CompilerParams(vmem_limit_bytes=40 * MIB),
        cost_estimate=pl.CostEstimate(
            flops=2 * cols * total * width, bytes_accessed=24 * cols * width, transcendentals=cols * width
        ),
        name="update",
    )(in_vmem(transport), in_hbm(emb), scale, centroids, first_moment, second_moment)


def over(axis, size, mask):
    return functools.partial(lax.ppermute, axis_name=axis, perm=[(i, i ^ mask) for i in range(size)])


def all_sum(value, dp, combine):
    value = combine([value, over("cent", 4, 1)(value)])
    plane = [value, over("cent", 4, 2)(value), over("dp", dp, 1)(value)]
    both = lax.ppermute(value, ("dp", "cent"), [(d * 4 + k, (d ^ 1) * 4 + (k ^ 2)) for d in range(dp) for k in range(4)])
    value = combine(plane + [both])
    line = [value] + [over("dp", dp, 2 * m)(value) for m in range(1, dp // 2)]
    return combine(line)


def add_up(parts):
    return functools.reduce(lambda a, b: a + b, parts)


def log_add_up(parts):
    top = functools.reduce(jnp.maximum, parts)
    return top + jnp.log2(add_up([jnp.exp2(q - top) for q in parts]))


def gathered(stream, sample_index, centroids, first_moment, second_moment):
    dp, cent = lax.axis_size("dp"), lax.axis_size("cent")
    local = sample_index.shape[0]
    cols = centroids.shape[0]
    total = local * dp
    band = cols * dp * cent
    half = local // 2
    p = (half * 11 // 32) // 16 * 16
    a = half - p
    k = lax.axis_index("cent")
    x, c = k // 2, k % 2
    d = lax.axis_index("dp")
    line = dp // 2
    order = [2 * i for i in range(line)] + [2 * i + 1 for i in reversed(range(line))]
    spot = jnp.where(d % 2 == 0, d // 2, dp - 1 - d // 2)

    def shard_at(place):
        place = place % dp
        return jnp.where(place < line, 2 * place, 2 * (dp - 1 - place) + 1)

    def take(index):
        return stream.at[index].get(mode="promise_in_bounds")

    hops = [(order[i], order[(i + 1) % dp]) for i in range(dp)]
    ahead = functools.partial(lax.ppermute, axis_name="dp", perm=hops)
    back = functools.partial(lax.ppermute, axis_name="dp", perm=[(j, i) for i, j in hops])
    across, core = over("cent", cent, 2), over("cent", cent, 1)

    mine = take(
        jnp.concatenate(
            [lax.dynamic_slice(sample_index, (c * half + x * p,), (p,)), lax.dynamic_slice(sample_index, (c * half + 2 * p,), (a - p,))]
        )
    )
    fore, aft = ahead(mine), back(mine)
    own = take(sample_index)
    rounded = centroids.astype(jnp.bfloat16)
    sq = jnp.sum(rounded.astype(jnp.float32) ** 2, axis=1, keepdims=True) / temper

    score = functools.partial(scores, half=half, p=p, cents=rounded, sq=sq, total=total)
    zero = jnp.zeros((), jnp.int32)
    held = score([own], [(0, 0, 2 * half, 0, False, "whole")], jnp.stack([d, d, zero, zero]))
    waiting = None
    for step in range(1, line + 1):
        last = step == line
        if waiting is not None:
            fore, aft, lse = lax.optimization_barrier((fore, aft, held[2]))
            held = (held[0], held[1], lse)
        slots = [shard_at(spot - step), shard_at(spot + step)]
        if last:
            far = across(fore)
            pieces = [fore, aft, far]
            near = [(0, 0, p, 0, "near"), (1, 0, a - p, 0, "shared"), (2, 0, p, 0, "far")]
        else:
            cut = step == line - 1
            send = (fore[:p], aft[p:]) if cut else (fore, aft)
            next_fore, next_aft = ahead(send[0]), back(send[1])
            far = across(jnp.concatenate([fore[:p], aft[:p]], axis=0))
            pieces = [fore, aft, far]
            near = [(i, 0, p, i, "near") for i in range(2)] + [(i, p, a - p, i, "shared") for i in range(2)]
            near += [(2, i * p, p, i, "far") for i in range(2)]
        pieces = pieces + [core(q) for q in pieces]
        segments = [(q + 3 * sib, start, rows, to, bool(sib), kind) for q, start, rows, to, kind in near for sib in range(2)]
        if waiting is not None:
            held = score(*waiting, held=held)
        waiting = (pieces, segments, jnp.stack(slots + [x, c]))
        if not last:
            fore, aft = next_fore, next_aft
    emb, logits, lse = score(*waiting, held=held)

    share = math.log2(total / band)
    u = -all_sum(lse.reshape(total), dp, log_add_up)
    v = jnp.zeros((cols, 1), jnp.float32)
    for sweep in range(ITERS):
        v, r, *kept = balance(sweep == 0, sweep == ITERS - 1, share, logits, u.reshape(1, total), v)
        logits = kept[0] if kept else logits
        rows = all_sum(r.reshape(total), dp, add_up)
        if sweep < ITERS - 1:
            u = u - jnp.log2(rows)
    scale = (1.0 / rows).reshape(1, total)
    return tuple(update(band / total, logits, emb, scale, centroids, first_moment, second_moment))


def scattered(stream, sample_index, centroids, first_moment, second_moment):
    embedded = stream[sample_index]
    total_rows = embedded.shape[0] * lax.axis_size("dp")
    band = centroids.shape[0] * lax.axis_size("dp") * lax.axis_size("cent")
    balance_of = math.log(total_rows / band)
    rounded = centroids.astype(jnp.bfloat16)
    shard_piece = lax.all_gather(rounded, "dp", axis=0, tiled=True)
    squares = jnp.sum(shard_piece.astype(jnp.float32) ** 2, axis=1)
    product = lax.dot_general(embedded, shard_piece, (((1,), (1,)), ((), ())), preferred_element_type=jnp.float32)
    logits = (2.0 * product - squares[None, :]) / temper

    def potential(shifted, axis, name):
        highest = jnp.max(shifted, axis=axis, keepdims=True)
        summed = jnp.sum(jnp.exp(shifted - highest), axis=axis, keepdims=True)
        overall = lax.pmax(highest, name)
        return -(overall + jnp.log(lax.psum(summed * jnp.exp(highest - overall), name)))

    column_pot = jnp.zeros((1, logits.shape[1]), jnp.float32)
    for _ in range(ITERS):
        row_pot = potential(logits + column_pot, 1, "cent")
        column_pot = balance_of + potential(logits + row_pot, 0, "dp")
    row_pot = potential(logits + column_pot, 1, "cent")
    transport = jnp.exp(logits + row_pot + column_pot).astype(jnp.bfloat16)
    weighted = lax.dot_general(transport, embedded, (((0,), (0,)), ((), ())), preferred_element_type=jnp.float32)
    weight_mass = jnp.sum(transport.astype(jnp.float32), axis=0)
    weighted = lax.psum_scatter(weighted, "dp", scatter_dimension=0, tiled=True)
    weight_mass = lax.psum_scatter(weight_mass, "dp", scatter_dimension=0, tiled=True)
    gradient = (weight_mass[:, None] * centroids - weighted) * (band / total_rows)
    new_first = beta_one * first_moment + (1.0 - beta_one) * gradient
    new_second = beta_two * second_moment + (1.0 - beta_two) * gradient * gradient
    new_centroids = centroids - step_rate * new_first / (jnp.sqrt(new_second) + epsilon)
    return (new_centroids, new_first, new_second)


def solution(mesh):
    small = mesh.shape["dp"] == 8 and mesh.shape["cent"] == 4
    return jax.shard_map(
        gathered if small else scattered,
        mesh=mesh,
        in_specs=(
            P("dp", None),
            P("dp"),
            P(("cent", "dp"), None),
            P(("cent", "dp"), None),
            P(("cent", "dp"), None),
        ),
        out_specs=(P(("cent", "dp"), None), P(("cent", "dp"), None), P(("cent", "dp"), None)),
        check_vma=False,
    )
```
